32 devices in a mesh: past: 4 (over y, x), second: 8 (over z, core).
Axes of the slice: x: 2, y: 2, z: 4, core: 2. Of those that a mesh axis runs over, the one named last changes fastest.
Arguments:
- resident: bfloat16 [12288, 12288], P('past', 'second'), may hold values from -6 to 6
- memory: bfloat16 [2, 384, 12288], P(None, None, 'past'), may hold values from -0.0546875 to 0.0546875
- previous: bfloat16 [2, 384, 12288], P(None, None, 'second'), may hold values from -6 to 6
- inverse_part: float32 [2, 384, 384], replicated, may hold values from -0.3125 to 0.3125
- pair_coupling: float32 [32, 32], replicated, may hold values from 0.0004510549 to 0.004510549
Outputs:
- fronts: bfloat16 [2, 384, 12288], P(None, None, 'second')
The draws below stay inside these ranges and needn't reach their ends.
All inputs are finite; a program needn't handle non-finite values.
Results may differ from the reference program's by a relative error of at most 0.017.
Values may be sent and summed in bfloat16 or wider, within the bound.
A program may use at most 128 MiB of HBM per device.

```python
import math
import jax
import jax.numpy as jnp
from jax import lax

ORB = 32
ROWS = 384
COLS = 12288
PAST = 12288
N_PAST = 4


def block_scale(own_key, extent, shards, low, top_value):
    level = 1.0
    for dim, blocks in shards:
        draws = jax.random.uniform(jax.random.fold_in(jax.random.fold_in(own_key, 6), dim), (blocks,), jnp.float32, low / len(shards), top_value / len(shards))
        level = level * jnp.repeat(jnp.exp(draws), extent[dim] // blocks).reshape((-1,) + (1,) * (len(extent) - 1 - dim))
    return level


def centred(rng, dims, spread, reach, cuts=(), dtype=jnp.bfloat16):
    array = spread * jax.random.normal(rng, dims, jnp.float32)
    if cuts:
        array = array * block_scale(rng, dims, cuts, -0.22, 0.18)
    return jnp.clip(array, -reach, reach).astype(dtype)


def setup_inputs(seed: int = 0) -> dict:
    key_of = jax.random.split(jax.random.key(seed), 6)
    return {
        "resident": centred(key_of[0], (PAST, COLS), 1.0, 6.0, ((0, 4), (1, 8))),
        "memory": centred(key_of[1], (2, ROWS, PAST), PAST ** -0.5, 0.0546875, ((2, 4),)),
        "previous": centred(key_of[2], (2, ROWS, COLS), 1.0, 6.0, ((2, 8),)),
        "inverse_part": centred(key_of[3], (2, ROWS, ROWS), ROWS ** -0.5, 0.3125, (), jnp.float32),
        "pair_coupling": jnp.clip(jnp.exp(jax.random.uniform(key_of[4], (ORB, ORB), jnp.float32, math.log(0.0004510549), math.log(0.004510549))), 0.0004510549, 0.004510549),
    }


step_size = 0.5


def orbital_flip(block, orbitals):
    row_count, col_count = block.shape
    blocks = block.reshape(row_count // orbitals, orbitals, col_count // orbitals, orbitals)
    return blocks.transpose(0, 3, 2, 1).reshape(row_count, col_count)


def history(memory_row, resident):
    depth = PAST // N_PAST
    slabs = resident.reshape(N_PAST, depth, COLS)
    pieces = memory_row.reshape(ROWS, N_PAST, depth).transpose(1, 0, 2)

    def add_term(total, pair):
        term = jnp.dot(pair[0], pair[1], preferred_element_type=jnp.float32)
        rounded = lax.optimization_barrier(term.astype(jnp.bfloat16))
        return total + rounded.astype(jnp.float32), None

    total, _ = lax.scan(add_term, jnp.zeros((ROWS, COLS), jnp.float32), (pieces, slabs))
    return total


def solve_front(summed, prior, inverse_block):
    source = prior.astype(jnp.float32) - step_size * summed
    solved = source + jnp.dot(inverse_block, source, precision=lax.Precision.HIGHEST, preferred_element_type=jnp.float32)
    return solved.astype(jnp.bfloat16)


def self_energy(front, pair_coupling):
    values = front.astype(jnp.float32)
    mirror = orbital_flip(values, ORB)
    blocks = (values * values * mirror).reshape(ROWS // ORB, ORB, COLS // ORB, ORB)
    return (blocks * pair_coupling[None, :, None, :]).reshape(ROWS, COLS).astype(jnp.bfloat16)


def reference(resident, memory, previous, inverse_part, pair_coupling):
    front_one = solve_front(history(memory[0], resident), previous[0], inverse_part[0])
    energy = self_energy(front_one, pair_coupling)
    memory_next = (memory[1].astype(jnp.float32) + orbital_flip(energy, ORB).astype(jnp.float32)).astype(jnp.bfloat16)
    front_two = solve_front(history(memory_next, resident), previous[1], inverse_part[1])
    return jnp.stack([front_one, front_two])
```

```python
import functools

import jax
import jax.numpy as jnp
from jax import lax
from jax.experimental import pallas as pl
from jax.experimental.pallas import tpu as pltpu
from jax.sharding import PartitionSpec as P

step_size = 0.5
MESH = pl.DeviceIdType.MESH
LANES = 128
CORES = 2


def orbital_flip(block, orbitals):
    row_count, col_count = block.shape
    blocks = block.reshape(row_count // orbitals, orbitals, col_count // orbitals, orbitals)
    return blocks.transpose(0, 3, 2, 1).reshape(row_count, col_count)


def solve_front(summed, prior, inverse_block):
    source = prior.astype(jnp.float32) - step_size * summed
    solved = source + jnp.dot(
        inverse_block, source, precision=lax.Precision.HIGHEST, preferred_element_type=jnp.float32
    )
    return solved.astype(jnp.bfloat16)


def self_energy(front, pair_coupling):
    orbitals = pair_coupling.shape[0]
    row_count, col_count = front.shape
    values = front.astype(jnp.float32)
    mirror = orbital_flip(values, orbitals)
    blocks = (values * values * mirror).reshape(
        row_count // orbitals, orbitals, col_count // orbitals, orbitals
    )
    return (
        (blocks * pair_coupling[None, :, None, :])
        .reshape(row_count, col_count)
        .astype(jnp.bfloat16)
    )


def per_device_plain(resident, memory, previous, inverse_part, pair_coupling):
    past_count = lax.axis_size("past")

    def advance(memory_row, front_index):
        partial_value = jnp.dot(memory_row, resident, preferred_element_type=jnp.float32)
        summed = lax.psum(partial_value.astype(jnp.bfloat16), "past").astype(jnp.float32)
        return solve_front(summed, previous[front_index], inverse_part[front_index])

    front_one = advance(memory[0], 0)
    energy_one = self_energy(front_one, pair_coupling)
    band = energy_one.shape[0] // past_count
    own_rows = lax.dynamic_slice_in_dim(energy_one, lax.axis_index("past") * band, band, 0)
    wide_band = lax.all_gather(own_rows, "second", axis=1, tiled=True)
    gathered = lax.all_to_all(wide_band, "past", split_axis=1, concat_axis=0, tiled=True)
    memory_next = (
        memory[1].astype(jnp.float32)
        + orbital_flip(gathered, pair_coupling.shape[0]).astype(jnp.float32)
    ).astype(jnp.bfloat16)
    front_two = advance(memory_next, 1)
    return jnp.stack([front_one, front_two])


def flip_bit(index, mask):
    bit = 1
    while bit <= mask:
        if mask & bit:
            index = index + bit - 2 * bit * ((index // bit) % 2)
        bit *= 2
    return index


def flip_tile(tile, orbitals):
    size = tile.shape[0]
    turned = tile.T
    row_block = lax.broadcasted_iota(jnp.int32, tile.shape, 0) // orbitals
    col_block = lax.broadcasted_iota(jnp.int32, tile.shape, 1) // orbitals
    count = size // orbitals
    lag = (row_block - col_block + count) % count
    out = turned
    for d in range(1, count):
        moved = pltpu.roll(turned, d * orbitals, axis=0)
        moved = pltpu.roll(moved, size - d * orbitals, axis=1)
        out = jnp.where(lag == d, moved, out)
    return out


def kernel(
    n, resident, memory, previous, inverse, coupling, out,
    res, mem0, mem1, prev, inv, acc, sbuf, rsum, gbuf, front, ebuf, rbuf,
    res_sem, mem0_sem, mem1_sem, small_sem, out_sem,
    rs_send, rs_recv, ag_send, ag_recv,
    up_send, down_send, line_recv, plane_send, plane_recv, core_send, core_recv,
):
    me = lax.axis_index("past")
    second = lax.axis_index("second")
    place, core = second // CORES, second % CORES
    partner = place * CORES + 1 - core
    rows, share = sbuf.shape[2], sbuf.shape[3]
    orbitals = coupling.shape[0]
    highest = lax.Precision.HIGHEST

    def columns(index):
        return pl.ds(pl.multiple_of(index * share, LANES), share)

    load_mem0 = pltpu.make_async_copy(memory.at[0], mem0, mem0_sem)
    load_mem0.start()
    def load_res(q):
        return pltpu.make_async_copy(resident.at[:, columns(q)], res.at[q], res_sem.at[q])
    for i in range(n - 1, -1, -1):
        load_res(flip_bit(me, i)).start()
    load_prev = pltpu.make_async_copy(previous.at[:, :, columns(me)], prev, small_sem.at[0])
    load_inv = pltpu.make_async_copy(inverse, inv, small_sem.at[1])
    load_prev.start()
    load_inv.start()
    def load_mem1(k):
        return pltpu.make_async_copy(memory.at[1, :, columns(k)], mem1.at[k], mem1_sem.at[k])
    for k in range(CORES * n):
        load_mem1(k).start()

    barrier = pltpu.get_barrier_semaphore()
    for i in range(1, n):
        pl.semaphore_signal(barrier, inc=1, device_id={"past": flip_bit(me, i)}, device_id_type=MESH)
    pl.semaphore_signal(barrier, inc=1, device_id={"second": partner}, device_id_type=MESH)
    @pl.when(place > 0)
    def _():
        pl.semaphore_signal(barrier, inc=1, device_id={"second": second - CORES}, device_id_type=MESH)
    @pl.when(place < n - 1)
    def _():
        pl.semaphore_signal(barrier, inc=1, device_id={"second": second + CORES}, device_id_type=MESH)
    has_lower, has_upper = (place + n - 1) // n, (2 * (n - 1) - place) // n
    pl.semaphore_wait(barrier, n + has_lower + has_upper)

    def remote(src, dst, send, recv, **where):
        return pltpu.make_async_remote_copy(
            src_ref=src, dst_ref=dst, send_sem=send, recv_sem=recv,
            device_id=where, device_id_type=MESH,
        )

    def scatter(f, q):
        return remote(sbuf.at[f, q], rsum.at[f, me], rs_send.at[f, q], rs_recv.at[f, me], past=q)

    def scatter_arrival(f, q):
        return remote(sbuf.at[f, q], rsum.at[f, q], rs_send.at[f, q], rs_recv.at[f, q], past=q)

    def gather(f, q):
        return remote(gbuf.at[f], out.at[f, :, columns(me)], ag_send.at[f, q], ag_recv.at[f, me], past=q)

    def gather_arrival(f, q):
        return remote(gbuf.at[f], out.at[f, :, columns(q)], ag_send.at[f, q], ag_recv.at[f, q], past=q)

    def keep(f):
        return pltpu.make_async_copy(gbuf.at[f], out.at[f, :, columns(me)], out_sem.at[f])

    def finish_front(f, own):
        total = own
        for i in range(1, n):
            q = flip_bit(me, i)
            scatter_arrival(f, q).wait_recv()
            total = total + rsum[f, q].astype(jnp.float32)
        source = prev[f].astype(jnp.float32) - step_size * total
        solved = source + jnp.dot(
            inv[f], source, precision=highest, preferred_element_type=jnp.float32
        )
        gbuf[f] = solved.astype(jnp.bfloat16)

    load_mem0.wait()
    own = None
    for i in range(n - 1, -1, -1):
        q = flip_bit(me, i)
        load_res(q).wait()
        term = jnp.dot(mem0[...], res[q], preferred_element_type=jnp.float32)
        if i:
            sbuf[0, q] = term.astype(jnp.bfloat16)
            scatter(0, q).start()
        else:
            acc[me] = term
    load_prev.wait()
    load_inv.wait()
    finish_front(0, acc[me])

    width = LANES
    spread = (
        lax.broadcasted_iota(jnp.int32, (width, orbitals), 0) % orbitals
        == lax.broadcasted_iota(jnp.int32, (width, orbitals), 1)
    ).astype(jnp.float32)
    half = lax.dot_general(spread, coupling[...], (((1,), (1,)), ((), ())),
                           precision=highest, preferred_element_type=jnp.float32)
    weight = lax.dot_general(half, spread, (((1,), (1,)), ((), ())),
                             precision=highest, preferred_element_type=jnp.float32)
    front[...] = gbuf[0].astype(jnp.float32)
    for r in range(rows // width):
        for s in range(share // width):
            at = (slice(r * width, (r + 1) * width), slice(s * width, (s + 1) * width))
            values = front[at]
            mirror = flip_tile(values, orbitals)
            ebuf[(place,) + at] = (mirror * mirror * values * weight).astype(jnp.bfloat16)

    def up(j):
        return remote(ebuf.at[j], ebuf.at[j], up_send.at[j], line_recv.at[j], second=second + CORES)

    def down(j):
        return remote(ebuf.at[j], ebuf.at[j], down_send.at[j], line_recv.at[j], second=second - CORES)

    def to_owner(j):
        return remote(ebuf.at[j], rbuf.at[core, me], plane_send.at[j], plane_recv.at[me], past=j)

    def owner_arrival(q):
        return remote(ebuf.at[q], rbuf.at[core, q], plane_send.at[q], plane_recv.at[q], past=q)

    def to_partner_own():
        return remote(ebuf.at[me], rbuf.at[core, me], core_send.at[me], core_recv.at[me], second=partner)

    def to_partner(q):
        return remote(rbuf.at[core, q], rbuf.at[core, q], core_send.at[q], core_recv.at[q], second=partner)

    def partner_arrival(q):
        return remote(rbuf.at[1 - core, q], rbuf.at[1 - core, q], core_send.at[q], core_recv.at[q], second=partner)

    def deliver(j):
        @pl.when(j != me)
        def _():
            to_owner(j).start()
        @pl.when(j == me)
        def _():
            to_partner_own().start()

    @pl.when(place < n - 1)
    def _():
        up(place).start()
    @pl.when(place > 0)
    def _():
        down(place).start()
    deliver(place)
    for k in range(1, n):
        @pl.when(place >= k)
        def _():
            j = place - k
            down(j).wait_recv()
            @pl.when(place < n - 1)
            def _():
                up(j).start()
            deliver(j)
        @pl.when(place + k < n)
        def _():
            j = place + k
            up(j).wait_recv()
            @pl.when(place > 0)
            def _():
                down(j).start()
            deliver(j)
    keep(0).start()
    for i in range(n - 1, 0, -1):
        gather(0, flip_bit(me, i)).start()
    for k in range(CORES * n):
        load_mem1(k).wait()

    def add_energy(k, energy):
        mem1[k] = (mem1[k].astype(jnp.float32) + energy.astype(jnp.float32)).astype(jnp.bfloat16)

    for i in range(n):
        q = flip_bit(me, i)
        mine, other = core * n + q, (1 - core) * n + q
        if i == 0:
            add_energy(mine, ebuf[me])
        else:
            owner_arrival(q).wait_recv()
            to_partner(q).start()
            add_energy(mine, rbuf[core, q])
        partner_arrival(q).wait_recv()
        add_energy(other, rbuf[1 - core, q])

        def term_of(c, i=i, q=q):
            term = None
            for k in (q, n + q):
                part = jnp.dot(
                    mem1[k], res[c, pl.ds(pl.multiple_of(k * share, LANES), share), :],
                    preferred_element_type=jnp.float32,
                )
                term = part if term is None else term + part
            return term if i == 0 else acc[c] + term

        if i < n - 1:
            @pl.loop(0, n)
            def _(c):
                acc[c] = term_of(c)
        else:
            for h in range(n - 1, 0, -1):
                c = flip_bit(me, h)
                sbuf[1, c] = term_of(c).astype(jnp.bfloat16)
                scatter(1, c).start()
            acc[me] = term_of(me)
    finish_front(1, acc[me])
    keep(1).start()
    for i in range(n - 1, 0, -1):
        gather(1, flip_bit(me, i)).start()

    for i in range(n):
        q = flip_bit(me, i)
        if i == 0:
            to_partner_own().wait_send()
        else:
            to_partner(q).wait_send()
            to_owner(q).wait_send()
            for f in range(2):
                scatter(f, q).wait_send()
                gather(f, q).wait_send()
                gather_arrival(f, q).wait_recv()
    for j in range(n):
        @pl.when((place < n - 1) & (place >= j))
        def _():
            up(j).wait_send()
        @pl.when((place > 0) & (place <= j))
        def _():
            down(j).wait_send()
    for f in range(2):
        keep(f).wait()


def per_device(resident, memory, previous, inverse_part, pair_coupling, n):
    depth, cols = resident.shape
    rows = memory.shape[1]
    share = cols // n
    bf16, f32 = jnp.bfloat16, jnp.float32
    dma = pltpu.SemaphoreType.DMA
    hbm = pl.BlockSpec(memory_space=pl.ANY)
    return pl.pallas_call(
        functools.partial(kernel, n),
        out_shape=jax.ShapeDtypeStruct(previous.shape, bf16),
        in_specs=[hbm, hbm, hbm, hbm, pl.BlockSpec(memory_space=pltpu.VMEM)],
        out_specs=hbm,
        scratch_shapes=[
            pltpu.VMEM((n, depth, share), bf16),
            pltpu.VMEM((rows, depth), bf16),
            pltpu.VMEM((CORES * n, rows, share), bf16),
            pltpu.VMEM((2, rows, share), bf16),
            pltpu.VMEM((2, rows, rows), f32),
            pltpu.VMEM((n, rows, share), f32),
            pltpu.VMEM((2, n, rows, share), bf16),
            pltpu.VMEM((2, n, rows, share), bf16),
            pltpu.VMEM((2, rows, share), bf16),
            pltpu.VMEM((rows, share), f32),
            pltpu.VMEM((n, rows, share), bf16),
            pltpu.VMEM((CORES, n, rows, share), bf16),
            dma((n,)), dma, dma((CORES * n,)), dma((2,)), dma((2,)),
            dma((2, n)), dma((2, n)), dma((2, n)), dma((2, n)),
            dma((n,)), dma((n,)), dma((n,)), dma((n,)), dma((n,)), dma((n,)), dma((n,)),
        ],
        compiler_params=pltpu.CompilerParams(
            collective_id=0, has_side_effects=True, vmem_limit_bytes=56 * 1024 * 1024
        ),
    )(resident, memory, previous, inverse_part, pair_coupling)


def solution(mesh):
    past, second = mesh.shape["past"], mesh.shape["second"]
    in_specs = (P("past", "second"), P(None, None, "past"), P(None, None, "second"), P(), P())
    out_specs = P(None, None, "second")

    def body(resident, memory, previous, inverse_part, pair_coupling):
        depth, cols = resident.shape
        orbitals = pair_coupling.shape[0]
        fits = (
            cols % (past * LANES) == 0
            and past & (past - 1) == 0
            and second == CORES * past
            and depth == CORES * cols
            and memory.shape[1] % LANES == 0
            and LANES % orbitals == 0
        )
        if fits:
            return per_device(resident, memory, previous, inverse_part, pair_coupling, past)
        return per_device_plain(resident, memory, previous, inverse_part, pair_coupling)

    return jax.shard_map(
        body, mesh=mesh, in_specs=in_specs, out_specs=out_specs, check_vma=False
    )
```

```python
import functools

import jax
import jax.numpy as jnp
from jax import lax
from jax.experimental import pallas as pl
from jax.experimental.pallas import tpu as pltpu
from jax.sharding import PartitionSpec as P

step_size = 0.5
MESH = pl.DeviceIdType.MESH
LANES = 128
CORES = 2


def orbital_flip(block, orbitals):
    row_count, col_count = block.shape
    blocks = block.reshape(row_count // orbitals, orbitals, col_count // orbitals, orbitals)
    return blocks.transpose(0, 3, 2, 1).reshape(row_count, col_count)


def solve_front(summed, prior, inverse_block):
    source = prior.astype(jnp.float32) - step_size * summed
    solved = source + jnp.dot(
        inverse_block, source, precision=lax.Precision.HIGHEST, preferred_element_type=jnp.float32
    )
    return solved.astype(jnp.bfloat16)


def self_energy(front, pair_coupling):
    orbitals = pair_coupling.shape[0]
    row_count, col_count = front.shape
    values = front.astype(jnp.float32)
    mirror = orbital_flip(values, orbitals)
    blocks = (values * values * mirror).reshape(
        row_count // orbitals, orbitals, col_count // orbitals, orbitals
    )
    return (
        (blocks * pair_coupling[None, :, None, :])
        .reshape(row_count, col_count)
        .astype(jnp.bfloat16)
    )


def per_device_plain(resident, memory, previous, inverse_part, pair_coupling):
    past_count = lax.axis_size("past")

    def advance(memory_row, front_index):
        partial_value = jnp.dot(memory_row, resident, preferred_element_type=jnp.float32)
        summed = lax.psum(partial_value.astype(jnp.bfloat16), "past").astype(jnp.float32)
        return solve_front(summed, previous[front_index], inverse_part[front_index])

    front_one = advance(memory[0], 0)
    energy_one = self_energy(front_one, pair_coupling)
    band = energy_one.shape[0] // past_count
    own_rows = lax.dynamic_slice_in_dim(energy_one, lax.axis_index("past") * band, band, 0)
    wide_band = lax.all_gather(own_rows, "second", axis=1, tiled=True)
    gathered = lax.all_to_all(wide_band, "past", split_axis=1, concat_axis=0, tiled=True)
    memory_next = (
        memory[1].astype(jnp.float32)
        + orbital_flip(gathered, pair_coupling.shape[0]).astype(jnp.float32)
    ).astype(jnp.bfloat16)
    front_two = advance(memory_next, 1)
    return jnp.stack([front_one, front_two])


def flip_bit(index, mask):
    bit = 1
    while bit <= mask:
        if mask & bit:
            index = index + bit - 2 * bit * ((index // bit) % 2)
        bit *= 2
    return index


def flip_tile(tile, orbitals):
    size = tile.shape[0]
    turned = tile.T
    row_block = lax.broadcasted_iota(jnp.int32, tile.shape, 0) // orbitals
    col_block = lax.broadcasted_iota(jnp.int32, tile.shape, 1) // orbitals
    count = size // orbitals
    lag = (row_block - col_block + count) % count
    out = turned
    for d in range(1, count):
        moved = pltpu.roll(turned, d * orbitals, axis=0)
        moved = pltpu.roll(moved, size - d * orbitals, axis=1)
        out = jnp.where(lag == d, moved, out)
    return out


def kernel(
    n, resident, memory, previous, inverse, coupling, out,
    res, mem0, mem1, prev, inv, split, acc, sbuf, rsum, gbuf, front, ebuf, rbuf,
    res_sem, mem0_sem, mem1_sem, small_sem, out_sem,
    rs_send, rs_recv, ag_send, ag_recv,
    up_send, down_send, line_recv, plane_send, plane_recv, core_send, core_recv,
):
    me = lax.axis_index("past")
    second = lax.axis_index("second")
    place, core = second // CORES, second % CORES
    partner = place * CORES + 1 - core
    rows, share = front.shape
    orbitals = coupling.shape[0]
    half = rows // 2
    pieces = rows // LANES
    highest = lax.Precision.HIGHEST
    near = (flip_bit(me, 1), flip_bit(me, 2))
    far = flip_bit(me, 3)

    def columns(index):
        return pl.ds(pl.multiple_of(index * share, LANES), share)

    def part(h):
        return pl.ds(h * half, half)

    load_mem0 = pltpu.make_async_copy(memory.at[0], mem0, mem0_sem)
    load_mem0.start()
    def load_res(q):
        return pltpu.make_async_copy(resident.at[:, columns(q)], res.at[q], res_sem.at[q])
    for q in (far, *near, me):
        load_res(q).start()
    load_prev = pltpu.make_async_copy(previous.at[:, :, columns(me)], prev, small_sem.at[0])
    load_inv = pltpu.make_async_copy(inverse, inv, small_sem.at[1])
    load_prev.start()
    load_inv.start()
    def load_mem1(k):
        return pltpu.make_async_copy(memory.at[1, :, columns(k)], mem1.at[k], mem1_sem.at[k])
    for k in range(CORES * n):
        load_mem1(k).start()

    barrier = pltpu.get_barrier_semaphore()
    for q in (far, *near):
        pl.semaphore_signal(barrier, inc=1, device_id={"past": q}, device_id_type=MESH)
    pl.semaphore_signal(barrier, inc=1, device_id={"second": partner}, device_id_type=MESH)
    @pl.when(place > 0)
    def _():
        pl.semaphore_signal(barrier, inc=1, device_id={"second": second - CORES}, device_id_type=MESH)
    @pl.when(place < n - 1)
    def _():
        pl.semaphore_signal(barrier, inc=1, device_id={"second": second + CORES}, device_id_type=MESH)
    has_lower, has_upper = (place + n - 1) // n, (2 * (n - 1) - place) // n
    pl.semaphore_wait(barrier, n + has_lower + has_upper)

    def remote(src, dst, send, recv, **where):
        return pltpu.make_async_remote_copy(
            src_ref=src, dst_ref=dst, send_sem=send, recv_sem=recv,
            device_id=where, device_id_type=MESH,
        )

    def scatter(f, link, m):
        return remote(sbuf.at[f, link, m], rsum.at[f, link, m], rs_send.at[f, link, m],
                      rs_recv.at[f, link, m], past=near[link])

    def reduce_scatter(f, term):
        value = term(far)
        for link in range(2):
            sbuf[f, link, 0] = value[link * half:(link + 1) * half].astype(jnp.bfloat16)
            scatter(f, link, 0).start()
        for link in range(2):
            q = near[link]
            acc[q] = term(q)
            sbuf[f, link, 1] = acc[q, part(link), :].astype(jnp.bfloat16)
            scatter(f, link, 1).start()
        for link in range(2):
            other = 1 - link
            scatter(f, other, 0).wait_recv()
            sbuf[f, link, 2] = (
                acc[near[link], part(other), :] + rsum[f, other, 0].astype(jnp.float32)
            ).astype(jnp.bfloat16)
            scatter(f, link, 2).start()
        acc[me] = term(me)

    def finish_front(f):
        for link in range(2):
            scatter(f, link, 1).wait_recv()
            scatter(f, link, 2).wait_recv()
        for h in range(2):
            total = (
                acc[me, part(h), :]
                + rsum[f, h, 1].astype(jnp.float32)
                + rsum[f, 1 - h, 2].astype(jnp.float32)
            )
            front[part(h), :] = prev[f, part(h), :].astype(jnp.float32) - step_size * total
        source = front[...]
        high = source.astype(jnp.bfloat16)
        low = (source - high.astype(jnp.float32)).astype(jnp.bfloat16)
        dot = functools.partial(jnp.dot, preferred_element_type=jnp.float32)
        moved = dot(split[f, 0], high) + (dot(split[f, 0], low) + dot(split[f, 1], high))
        gbuf[f] = (source + moved).astype(jnp.bfloat16)

    def gather(f, link, m):
        if m < 2:
            h, q = (link, 1 - link)[m], me
            src = gbuf.at[f, part(h), :]
        else:
            h, q = 1 - link, near[1 - link]
            src = out.at[f, part(h), columns(q)]
        return remote(src, out.at[f, part(h), columns(q)], ag_send.at[f, link, m],
                      ag_recv.at[f, link, m], past=near[link])

    def gather_arrival(f, link, m):
        h = link if m == 0 else 1 - link
        q = far if m == 2 else near[link]
        ref = out.at[f, part(h), columns(q)]
        return remote(ref, ref, ag_send.at[f, link, m], ag_recv.at[f, link, m], past=near[link])

    def keep(f):
        return pltpu.make_async_copy(gbuf.at[f], out.at[f, :, columns(me)], out_sem.at[f])

    def gather_own(f):
        for m in range(2):
            for link in range(2):
                gather(f, link, m).start()
        keep(f).start()

    def gather_relay(f):
        for link in range(2):
            gather_arrival(f, 1 - link, 0).wait_recv()
            gather(f, link, 2).start()

    load_mem0.wait()
    def first_term(q):
        load_res(q).wait()
        return jnp.dot(mem0[...], res[q], preferred_element_type=jnp.float32)
    reduce_scatter(0, first_term)

    load_prev.wait()
    load_inv.wait()
    for f in range(2):
        value = inv[f]
        high = value.astype(jnp.bfloat16)
        split[f, 0] = high
        split[f, 1] = (value - high.astype(jnp.float32)).astype(jnp.bfloat16)
    spread = (
        lax.broadcasted_iota(jnp.int32, (LANES, orbitals), 0) % orbitals
        == lax.broadcasted_iota(jnp.int32, (LANES, orbitals), 1)
    ).astype(jnp.float32)
    tall = lax.dot_general(spread, coupling[...], (((1,), (1,)), ((), ())),
                           precision=highest, preferred_element_type=jnp.float32)
    weight = lax.dot_general(tall, spread, (((1,), (1,)), ((), ())),
                             precision=highest, preferred_element_type=jnp.float32)
    finish_front(0)

    def to_owner(s):
        return remote(ebuf.at[s], rbuf.at[core, me, s], plane_send.at[s], plane_recv.at[me, s], past=place)

    def owner_arrival(q, s):
        return remote(ebuf.at[s], rbuf.at[core, q, s], plane_send.at[s], plane_recv.at[q, s], past=q)

    for s in range(pieces):
        for c in range(share // LANES):
            at = (pl.ds(s * LANES, LANES), pl.ds(c * LANES, LANES))
            values = gbuf[(0,) + at].astype(jnp.float32)
            mirror = flip_tile(values, orbitals)
            ebuf[s, :, pl.ds(c * LANES, LANES)] = (mirror * mirror * values * weight).astype(jnp.bfloat16)
        @pl.when(me != place)
        def _():
            to_owner(s).start()
        @pl.when(me == place)
        def _():
            rbuf[core, me, s] = ebuf[s]
    gather_own(0)
    for k in range(CORES * n):
        load_mem1(k).wait()

    def up(q, s):
        return remote(rbuf.at[core, q, s], rbuf.at[core, q, s], up_send.at[q, s],
                      line_recv.at[q, s], second=second + CORES)

    def down(q, s):
        return remote(rbuf.at[core, q, s], rbuf.at[core, q, s], down_send.at[q, s],
                      line_recv.at[q, s], second=second - CORES)

    def across(q, s):
        return remote(rbuf.at[core, q, s], rbuf.at[core, q, s], core_send.at[q, s],
                      core_recv.at[q, s], second=partner)

    def across_arrival(q, s):
        ref = rbuf.at[1 - core, q, s]
        return remote(ref, ref, core_send.at[q, s], core_recv.at[q, s], second=partner)

    def pass_on(i, s):
        q = (me, *near, far)[i]
        if i:
            @pl.when(me == place)
            def _():
                owner_arrival(q, s).wait_recv()
        @pl.when(place > me)
        def _():
            down(q, s).wait_recv()
        @pl.when(place < me)
        def _():
            up(q, s).wait_recv()
        @pl.when((place >= me) & (place < n - 1))
        def _():
            up(q, s).start()
        @pl.when((place <= me) & (place > 0))
        def _():
            down(q, s).start()
        across(q, s).start()

    def add_energy(q):
        for side, is_partner in ((core, False), (1 - core, True)):
            for s in range(pieces):
                if is_partner:
                    across_arrival(q, s).wait_recv()
                at = (side * n + q, pl.ds(s * LANES, LANES))
                mem1[at] = (
                    mem1[at].astype(jnp.float32) + rbuf[side, q, s].astype(jnp.float32)
                ).astype(jnp.bfloat16)

    def second_term(q, c, first):
        term = None
        for k in (q, n + q):
            product = jnp.dot(
                mem1[k], res[c, pl.ds(pl.multiple_of(k * share, LANES), share), :],
                preferred_element_type=jnp.float32,
            )
            term = product if term is None else term + product
        return term if first else acc[c] + term

    for i in range(n):
        for s in range(pieces):
            pass_on(i, s)
            if i:
                q = (me, *near, far)[i - 1]
                if s == 0:
                    add_energy(q)
                for c in range(n):
                    if c * pieces // n == s:
                        acc[c] = second_term(q, c, i == 1)
    gather_relay(0)
    add_energy(far)
    reduce_scatter(1, lambda c: second_term(far, c, False))
    finish_front(1)
    gather_own(1)
    gather_relay(1)

    for f in range(2):
        for link in range(2):
            for m in range(3):
                scatter(f, link, m).wait_send()
                gather(f, link, m).wait_send()
                if m:
                    gather_arrival(f, link, m).wait_recv()
        keep(f).wait()
    for s in range(pieces):
        @pl.when(me != place)
        def _():
            to_owner(s).wait_send()
        for q in range(n):
            across(q, s).wait_send()
            @pl.when((place >= me) & (place < n - 1))
            def _():
                up(q, s).wait_send()
            @pl.when((place <= me) & (place > 0))
            def _():
                down(q, s).wait_send()


def per_device(resident, memory, previous, inverse_part, pair_coupling, n):
    depth, cols = resident.shape
    rows = memory.shape[1]
    share = cols // n
    pieces = rows // LANES
    bf16, f32 = jnp.bfloat16, jnp.float32
    dma = pltpu.SemaphoreType.DMA
    hbm = pl.BlockSpec(memory_space=pl.ANY)
    return pl.pallas_call(
        functools.partial(kernel, n),
        out_shape=jax.ShapeDtypeStruct(previous.shape, bf16),
        in_specs=[hbm, hbm, hbm, hbm, pl.BlockSpec(memory_space=pltpu.VMEM)],
        out_specs=hbm,
        scratch_shapes=[
            pltpu.VMEM((n, depth, share), bf16),
            pltpu.VMEM((rows, depth), bf16),
            pltpu.VMEM((CORES * n, rows, share), bf16),
            pltpu.VMEM((2, rows, share), bf16),
            pltpu.VMEM((2, rows, rows), f32),
            pltpu.VMEM((2, 2, rows, rows), bf16),
            pltpu.VMEM((n, rows, share), f32),
            pltpu.VMEM((2, 2, 3, rows // 2, share), bf16),
            pltpu.VMEM((2, 2, 3, rows // 2, share), bf16),
            pltpu.VMEM((2, rows, share), bf16),
            pltpu.VMEM((rows, share), f32),
            pltpu.VMEM((pieces, LANES, share), bf16),
            pltpu.VMEM((CORES, n, pieces, LANES, share), bf16),
            dma((n,)), dma, dma((CORES * n,)), dma((2,)), dma((2,)),
            dma((2, 2, 3)), dma((2, 2, 3)), dma((2, 2, 3)), dma((2, 2, 3)),
            dma((n, pieces)), dma((n, pieces)), dma((n, pieces)), dma((pieces,)),
            dma((n, pieces)), dma((n, pieces)), dma((n, pieces)),
        ],
        compiler_params=pltpu.CompilerParams(
            collective_id=0, has_side_effects=True, vmem_limit_bytes=56 * 1024 * 1024
        ),
    )(resident, memory, previous, inverse_part, pair_coupling)


def solution(mesh):
    past, second = mesh.shape["past"], mesh.shape["second"]
    in_specs = (P("past", "second"), P(None, None, "past"), P(None, None, "second"), P(), P())
    out_specs = P(None, None, "second")

    def body(resident, memory, previous, inverse_part, pair_coupling):
        depth, cols = resident.shape
        orbitals = pair_coupling.shape[0]
        fits = (
            cols % (past * LANES) == 0
            and past == 2 * 2
            and second == CORES * past
            and depth == CORES * cols
            and memory.shape[1] % (2 * LANES) in (0, LANES)
            and LANES % orbitals == 0
        )
        if fits:
            return per_device(resident, memory, previous, inverse_part, pair_coupling, past)
        return per_device_plain(resident, memory, previous, inverse_part, pair_coupling)

    return jax.shard_map(
        body, mesh=mesh, in_specs=in_specs, out_specs=out_specs, check_vma=False
    )
```

```python
import functools

import jax
import jax.numpy as jnp
from jax import lax
from jax.experimental import pallas as pl
from jax.experimental.pallas import tpu as pltpu
from jax.sharding import PartitionSpec as P

step_size = 0.5
MESH = pl.DeviceIdType.MESH
LANES = 128
CORES = 2
BAND = 64


def orbital_flip(block, orbitals):
    row_count, col_count = block.shape
    blocks = block.reshape(row_count // orbitals, orbitals, col_count // orbitals, orbitals)
    return blocks.transpose(0, 3, 2, 1).reshape(row_count, col_count)


def solve_front(summed, prior, inverse_block):
    source = prior.astype(jnp.float32) - step_size * summed
    solved = source + jnp.dot(
        inverse_block, source, precision=lax.Precision.HIGHEST, preferred_element_type=jnp.float32
    )
    return solved.astype(jnp.bfloat16)


def self_energy(front, pair_coupling):
    orbitals = pair_coupling.shape[0]
    row_count, col_count = front.shape
    values = front.astype(jnp.float32)
    mirror = orbital_flip(values, orbitals)
    blocks = (values * values * mirror).reshape(
        row_count // orbitals, orbitals, col_count // orbitals, orbitals
    )
    return (
        (blocks * pair_coupling[None, :, None, :])
        .reshape(row_count, col_count)
        .astype(jnp.bfloat16)
    )


def per_device_plain(resident, memory, previous, inverse_part, pair_coupling):
    past_count = lax.axis_size("past")

    def advance(memory_row, front_index):
        partial_value = jnp.dot(memory_row, resident, preferred_element_type=jnp.float32)
        summed = lax.psum(partial_value.astype(jnp.bfloat16), "past").astype(jnp.float32)
        return solve_front(summed, previous[front_index], inverse_part[front_index])

    front_one = advance(memory[0], 0)
    energy_one = self_energy(front_one, pair_coupling)
    band = energy_one.shape[0] // past_count
    own_rows = lax.dynamic_slice_in_dim(energy_one, lax.axis_index("past") * band, band, 0)
    wide_band = lax.all_gather(own_rows, "second", axis=1, tiled=True)
    gathered = lax.all_to_all(wide_band, "past", split_axis=1, concat_axis=0, tiled=True)
    memory_next = (
        memory[1].astype(jnp.float32)
        + orbital_flip(gathered, pair_coupling.shape[0]).astype(jnp.float32)
    ).astype(jnp.bfloat16)
    front_two = advance(memory_next, 1)
    return jnp.stack([front_one, front_two])


def flip_bit(index, mask):
    bit = 1
    while bit <= mask:
        if mask & bit:
            index = index + bit - 2 * bit * ((index // bit) % 2)
        bit *= 2
    return index


def flip_tile(tile, orbitals):
    size = tile.shape[0]
    turned = tile.T
    row_block = lax.broadcasted_iota(jnp.int32, tile.shape, 0) // orbitals
    col_block = lax.broadcasted_iota(jnp.int32, tile.shape, 1) // orbitals
    count = size // orbitals
    lag = (row_block - col_block + count) % count
    out = turned
    for d in range(1, count):
        moved = pltpu.roll(turned, d * orbitals, axis=0)
        moved = pltpu.roll(moved, size - d * orbitals, axis=1)
        out = jnp.where(lag == d, moved, out)
    return out


def kernel(
    n, resident, memory, previous, inverse, coupling, out,
    res, mem0, mem1, prev, inv, split, acc, sbuf, rsum, gbuf, front, ebuf, rbuf,
    res_sem, mem0_sem, mem1_sem, small_sem, out_sem,
    rs_send, rs_recv, ag_send, ag_recv,
    up_send, down_send, line_recv, plane_send, plane_recv, core_send, core_recv,
):
    me = lax.axis_index("past")
    second = lax.axis_index("second")
    place, core = second // CORES, second % CORES
    partner = place * CORES + 1 - core
    rows, share = front.shape
    orbitals = coupling.shape[0]
    half = rows // 2
    pieces = rows // BAND
    highest = lax.Precision.HIGHEST
    near = (flip_bit(me, 1), flip_bit(me, 2))
    far = flip_bit(me, 3)

    def columns(index):
        return pl.ds(pl.multiple_of(index * share, LANES), share)

    def part(h):
        return pl.ds(h * half, half)

    load_mem0 = pltpu.make_async_copy(memory.at[0], mem0, mem0_sem)
    load_mem0.start()
    def load_res(q):
        return pltpu.make_async_copy(resident.at[:, columns(q)], res.at[q], res_sem.at[q])
    for q in (far, *near, me):
        load_res(q).start()
    load_prev = pltpu.make_async_copy(previous.at[:, :, columns(me)], prev, small_sem.at[0])
    load_inv = pltpu.make_async_copy(inverse, inv, small_sem.at[1])
    load_prev.start()
    load_inv.start()
    def load_mem1(k):
        return pltpu.make_async_copy(memory.at[1, :, columns(k)], mem1.at[k], mem1_sem.at[k])
    for k in range(CORES * n):
        load_mem1(k).start()

    barrier = pltpu.get_barrier_semaphore()
    for q in (far, *near):
        pl.semaphore_signal(barrier, inc=1, device_id={"past": q}, device_id_type=MESH)
    pl.semaphore_signal(barrier, inc=1, device_id={"second": partner}, device_id_type=MESH)
    @pl.when(place > 0)
    def _():
        pl.semaphore_signal(barrier, inc=1, device_id={"second": second - CORES}, device_id_type=MESH)
    @pl.when(place < n - 1)
    def _():
        pl.semaphore_signal(barrier, inc=1, device_id={"second": second + CORES}, device_id_type=MESH)
    has_lower, has_upper = (place + n - 1) // n, (2 * (n - 1) - place) // n
    pl.semaphore_wait(barrier, n + has_lower + has_upper)

    def remote(src, dst, send, recv, **where):
        return pltpu.make_async_remote_copy(
            src_ref=src, dst_ref=dst, send_sem=send, recv_sem=recv,
            device_id=where, device_id_type=MESH,
        )

    def scatter(f, link, m):
        return remote(sbuf.at[f, link, m], rsum.at[f, link, m], rs_send.at[f, link, m],
                      rs_recv.at[f, link, m], past=near[link])

    def reduce_scatter(f, term):
        value = term(far)
        for link in range(2):
            sbuf[f, link, 0] = value[link * half:(link + 1) * half].astype(jnp.bfloat16)
            scatter(f, link, 0).start()
        for link in range(2):
            q = near[link]
            acc[q] = term(q)
            sbuf[f, link, 1] = acc[q, part(link), :].astype(jnp.bfloat16)
            scatter(f, link, 1).start()
        for link in range(2):
            other = 1 - link
            scatter(f, other, 0).wait_recv()
            sbuf[f, link, 2] = (
                acc[near[link], part(other), :] + rsum[f, other, 0].astype(jnp.float32)
            ).astype(jnp.bfloat16)
            scatter(f, link, 2).start()
        acc[me] = term(me)

    def finish_front(f):
        for link in range(2):
            scatter(f, link, 1).wait_recv()
            scatter(f, link, 2).wait_recv()
        for h in range(2):
            total = (
                acc[me, part(h), :]
                + rsum[f, h, 1].astype(jnp.float32)
                + rsum[f, 1 - h, 2].astype(jnp.float32)
            )
            front[part(h), :] = prev[f, part(h), :].astype(jnp.float32) - step_size * total
        source = front[...]
        high = source.astype(jnp.bfloat16)
        low = (source - high.astype(jnp.float32)).astype(jnp.bfloat16)
        dot = functools.partial(jnp.dot, preferred_element_type=jnp.float32)
        moved = dot(split[f, 0], high) + (dot(split[f, 0], low) + dot(split[f, 1], high))
        gbuf[f] = (source + moved).astype(jnp.bfloat16)

    def gather(f, link, m):
        if m < 2:
            h, q = (link, 1 - link)[m], me
            src = gbuf.at[f, part(h), :]
        else:
            h, q = 1 - link, near[1 - link]
            src = out.at[f, part(h), columns(q)]
        return remote(src, out.at[f, part(h), columns(q)], ag_send.at[f, link, m],
                      ag_recv.at[f, link, m], past=near[link])

    def gather_arrival(f, link, m):
        h = link if m == 0 else 1 - link
        q = far if m == 2 else near[link]
        ref = out.at[f, part(h), columns(q)]
        return remote(ref, ref, ag_send.at[f, link, m], ag_recv.at[f, link, m], past=near[link])

    def keep(f):
        return pltpu.make_async_copy(gbuf.at[f], out.at[f, :, columns(me)], out_sem.at[f])

    def gather_own(f):
        for m in range(2):
            for link in range(2):
                gather(f, link, m).start()
        keep(f).start()

    def gather_relay(f):
        for link in range(2):
            gather_arrival(f, 1 - link, 0).wait_recv()
            gather(f, link, 2).start()

    load_mem0.wait()
    def first_term(q):
        load_res(q).wait()
        return jnp.dot(mem0[...], res[q], preferred_element_type=jnp.float32)
    reduce_scatter(0, first_term)

    load_prev.wait()
    load_inv.wait()
    for f in range(2):
        value = inv[f]
        high = value.astype(jnp.bfloat16)
        split[f, 0] = high
        split[f, 1] = (value - high.astype(jnp.float32)).astype(jnp.bfloat16)
    spread = (
        lax.broadcasted_iota(jnp.int32, (LANES, orbitals), 0) % orbitals
        == lax.broadcasted_iota(jnp.int32, (LANES, orbitals), 1)
    ).astype(jnp.float32)
    tall = lax.dot_general(spread, coupling[...], (((1,), (1,)), ((), ())),
                           precision=highest, preferred_element_type=jnp.float32)
    weight = lax.dot_general(tall, spread, (((1,), (1,)), ((), ())),
                             precision=highest, preferred_element_type=jnp.float32)
    finish_front(0)

    def to_owner(s):
        return remote(ebuf.at[s], rbuf.at[core, me, s], plane_send.at[s], plane_recv.at[me, s], past=place)

    def owner_arrival(q, s):
        return remote(ebuf.at[s], rbuf.at[core, q, s], plane_send.at[s], plane_recv.at[q, s], past=q)

    bands = LANES // BAND
    for s in range(pieces):
        if s % bands == 0:
            for c in range(share // LANES):
                across_lanes = pl.ds(c * LANES, LANES)
                values = gbuf[0, pl.ds(s * BAND, LANES), across_lanes].astype(jnp.float32)
                mirror = flip_tile(values, orbitals)
                energy = (mirror * mirror * values * weight).astype(jnp.bfloat16)
                for u in range(bands):
                    ebuf[s + u, :, across_lanes] = energy[u * BAND:(u + 1) * BAND]
        @pl.when(me != place)
        def _():
            to_owner(s).start()
        @pl.when(me == place)
        def _():
            rbuf[core, me, s] = ebuf[s]
    gather_own(0)
    for k in range(CORES * n):
        load_mem1(k).wait()

    def up(q, s):
        return remote(rbuf.at[core, q, s], rbuf.at[core, q, s], up_send.at[q, s],
                      line_recv.at[q, s], second=second + CORES)

    def down(q, s):
        return remote(rbuf.at[core, q, s], rbuf.at[core, q, s], down_send.at[q, s],
                      line_recv.at[q, s], second=second - CORES)

    def across(q, s):
        return remote(rbuf.at[core, q, s], rbuf.at[core, q, s], core_send.at[q, s],
                      core_recv.at[q, s], second=partner)

    def across_arrival(q, s):
        ref = rbuf.at[1 - core, q, s]
        return remote(ref, ref, core_send.at[q, s], core_recv.at[q, s], second=partner)

    def pass_on(i, s):
        q = (me, *near, far)[i]
        if i:
            @pl.when(me == place)
            def _():
                owner_arrival(q, s).wait_recv()
        @pl.when(place > me)
        def _():
            down(q, s).wait_recv()
        @pl.when(place < me)
        def _():
            up(q, s).wait_recv()
        @pl.when((place >= me) & (place < n - 1))
        def _():
            up(q, s).start()
        @pl.when((place <= me) & (place > 0))
        def _():
            down(q, s).start()
        across(q, s).start()

    def add_energy(q):
        for side, is_partner in ((core, False), (1 - core, True)):
            for s in range(pieces):
                if is_partner:
                    across_arrival(q, s).wait_recv()
                at = (side * n + q, pl.ds(s * BAND, BAND))
                mem1[at] = (
                    mem1[at].astype(jnp.float32) + rbuf[side, q, s].astype(jnp.float32)
                ).astype(jnp.bfloat16)

    def second_term(q, c, first):
        term = None
        for k in (q, n + q):
            product = jnp.dot(
                mem1[k], res[c, pl.ds(pl.multiple_of(k * share, LANES), share), :],
                preferred_element_type=jnp.float32,
            )
            term = product if term is None else term + product
        return term if first else acc[c] + term

    for i in range(n):
        for s in range(pieces):
            pass_on(i, s)
            if i:
                q = (me, *near, far)[i - 1]
                if s == 0:
                    add_energy(q)
                for c in range(n):
                    if c * pieces // n == s:
                        acc[c] = second_term(q, c, i == 1)
    gather_relay(0)
    add_energy(far)
    reduce_scatter(1, lambda c: second_term(far, c, False))
    finish_front(1)
    gather_own(1)
    gather_relay(1)

    for f in range(2):
        for link in range(2):
            for m in range(3):
                scatter(f, link, m).wait_send()
                gather(f, link, m).wait_send()
                if m:
                    gather_arrival(f, link, m).wait_recv()
        keep(f).wait()
    for s in range(pieces):
        @pl.when(me != place)
        def _():
            to_owner(s).wait_send()
        for q in range(n):
            across(q, s).wait_send()
            @pl.when((place >= me) & (place < n - 1))
            def _():
                up(q, s).wait_send()
            @pl.when((place <= me) & (place > 0))
            def _():
                down(q, s).wait_send()


def per_device(resident, memory, previous, inverse_part, pair_coupling, n):
    depth, cols = resident.shape
    rows = memory.shape[1]
    share = cols // n
    pieces = rows // BAND
    bf16, f32 = jnp.bfloat16, jnp.float32
    dma = pltpu.SemaphoreType.DMA
    hbm = pl.BlockSpec(memory_space=pl.ANY)
    return pl.pallas_call(
        functools.partial(kernel, n),
        out_shape=jax.ShapeDtypeStruct(previous.shape, bf16),
        in_specs=[hbm, hbm, hbm, hbm, pl.BlockSpec(memory_space=pltpu.VMEM)],
        out_specs=hbm,
        scratch_shapes=[
            pltpu.VMEM((n, depth, share), bf16),
            pltpu.VMEM((rows, depth), bf16),
            pltpu.VMEM((CORES * n, rows, share), bf16),
            pltpu.VMEM((2, rows, share), bf16),
            pltpu.VMEM((2, rows, rows), f32),
            pltpu.VMEM((2, 2, rows, rows), bf16),
            pltpu.VMEM((n, rows, share), f32),
            pltpu.VMEM((2, 2, 3, rows // 2, share), bf16),
            pltpu.VMEM((2, 2, 3, rows // 2, share), bf16),
            pltpu.VMEM((2, rows, share), bf16),
            pltpu.VMEM((rows, share), f32),
            pltpu.VMEM((pieces, BAND, share), bf16),
            pltpu.VMEM((CORES, n, pieces, BAND, share), bf16),
            dma((n,)), dma, dma((CORES * n,)), dma((2,)), dma((2,)),
            dma((2, 2, 3)), dma((2, 2, 3)), dma((2, 2, 3)), dma((2, 2, 3)),
            dma((n, pieces)), dma((n, pieces)), dma((n, pieces)), dma((pieces,)),
            dma((n, pieces)), dma((n, pieces)), dma((n, pieces)),
        ],
        compiler_params=pltpu.CompilerParams(
            collective_id=0, has_side_effects=True, vmem_limit_bytes=56 * 1024 * 1024
        ),
    )(resident, memory, previous, inverse_part, pair_coupling)


def solution(mesh):
    past, second = mesh.shape["past"], mesh.shape["second"]
    in_specs = (P("past", "second"), P(None, None, "past"), P(None, None, "second"), P(), P())
    out_specs = P(None, None, "second")

    def body(resident, memory, previous, inverse_part, pair_coupling):
        depth, cols = resident.shape
        orbitals = pair_coupling.shape[0]
        fits = (
            cols % (past * LANES) == 0
            and past == 2 * 2
            and second == CORES * past
            and depth == CORES * cols
            and memory.shape[1] % (2 * LANES) in (0, LANES)
            and LANES % orbitals == 0
        )
        if fits:
            return per_device(resident, memory, previous, inverse_part, pair_coupling, past)
        return per_device_plain(resident, memory, previous, inverse_part, pair_coupling)

    return jax.shard_map(
        body, mesh=mesh, in_specs=in_specs, out_specs=out_specs, check_vma=False
    )
```
